32 devices in a mesh: wide: 16 (over z, y, x), tp: 2 (over core).
Axes of the slice: x: 2, y: 2, z: 4, core: 2. Of those that a mesh axis runs over, the one named last changes fastest.
Arguments:
- tokens: bfloat16 [6144, 2560], P(('wide', 'tp')), may hold values from -6 to 6
- positions: int32 [6144], P('wide'), may hold values from 0 to 2047, as said below
- norm1_gain: bfloat16 [2560], P('wide'), may hold values from 0.5 to 1.5
- query_weight: bfloat16 [2560, 2560], P('wide', 'tp'), may hold values from -0.125 to 0.125
- kv_weight: bfloat16 [2560, 512], P('wide'), may hold values from -0.125 to 0.125
- out_weight: bfloat16 [2560, 2560], P('wide', 'tp'), may hold values from -0.5 to 0.5
- norm2_gain: bfloat16 [2560], P('wide'), may hold values from 0.5 to 1.5
- gate_weight: bfloat16 [2560, 7680], P('wide', 'tp'), may hold values from -0.125 to 0.125
- up_weight: bfloat16 [2560, 7680], P('wide', 'tp'), may hold values from -0.125 to 0.125
- down_weight: bfloat16 [2560, 7680], P('wide', 'tp'), may hold values from -0.0625 to 0.0625
- cotangent: bfloat16 [6144, 2560], P(('wide', 'tp')), may hold values from -6 to 6
Outputs:
- output: bfloat16 [6144, 2560], P(('wide', 'tp'))
- grad_tokens: bfloat16 [6144, 2560], P(('wide', 'tp'))
- grad_norm1_gain: float32 [2560], P('wide')
- grad_query_weight: float32 [2560, 2560], P('wide', 'tp')
- grad_kv_weight: float32 [2560, 512], P('wide')
- grad_out_weight: float32 [2560, 2560], P('wide', 'tp')
- grad_norm2_gain: float32 [2560], P('wide')
- grad_gate_weight: float32 [2560, 7680], P('wide', 'tp')
- grad_up_weight: float32 [2560, 7680], P('wide', 'tp')
- grad_down_weight: float32 [2560, 7680], P('wide', 'tp')
The draws below stay inside these ranges and needn't reach their ends.
Inputs may be any that keep to these rules, and one draw needn't show every extreme that they name: Sequences lie end to end over the tokens; positions counts 0, 1, 2, ... through each sequence. Each sequence has 256 to 2048 tokens except the last, which may be cut by the end; some sequence has exactly 2048 tokens.
All inputs are finite; a program needn't handle non-finite values.
Results may differ from the reference program's by a relative error of at most 0.015.
Values may be sent and summed in bfloat16 or wider, within the bound.
No kernel may reach another device: no remote copies, remote signals or barrier semaphores. Data moves between devices by JAX's collectives and lax.ppermute only.
A program may use at most 320 MiB of HBM per device.

```python
import jax
import jax.numpy as jnp
from jax import lax

D = 2560
HQ = 10
HD = 256
FF = 7680
WINDOW = 2048
MAXLEN = 2048
MINSEQ = 256
TOK_W = 384
TOKENS = 6144
REACH = 6


def draw_positions(key, part):
    number = TOKENS // MINSEQ + 1
    lengths = jax.random.randint(jax.random.fold_in(key, 11), (number,), MINSEQ, MAXLEN + 1)
    longest = jax.random.randint(jax.random.fold_in(key, 12), (), 0, TOKENS // MAXLEN)
    lengths = jnp.where(jnp.arange(number) == longest, MAXLEN, lengths).astype(jnp.int32)
    finish = jnp.cumsum(lengths).astype(jnp.int32)
    starts = finish - lengths
    places = jnp.arange(TOKENS, dtype=jnp.int32)
    inside = (places[:, None] >= starts[None, :]) & (places[:, None] < finish[None, :])
    anchor = jnp.sum(jnp.where(inside, starts[None, :], 0), axis=1).astype(jnp.int32)
    return (places - anchor).astype(jnp.int32)


def raised(drawn, key, source, target, parts, factor):
    owner, partner = [(jnp.arange(drawn.shape[axis_at]) // (drawn.shape[axis_at] // parts)).reshape([-1 if axis == axis_at else 1 for axis in range(drawn.ndim)]) for axis_at in (source, target)]
    chosen = jax.random.permutation(key, parts)[partner]
    strong = (owner == chosen) | (owner == (partner + parts // 2) % parts)
    return jnp.where(strong, factor * drawn, drawn)


def steps_of(key, extent, cuts, least, top_value):
    gain, own = 1.0, jax.random.fold_in(key, 6)
    for axis_at, parts in cuts:
        draws = jnp.exp(jax.random.uniform(jax.random.fold_in(own, axis_at), (parts,), jnp.float32, least / len(cuts), top_value / len(cuts)))
        gain = gain * jnp.repeat(draws, extent[axis_at] // parts).reshape([-1 if axis == axis_at else 1 for axis in range(len(extent))])
    return gain


def gaussian(stream_key, dims, spread, bound, cuts=(), kind=jnp.bfloat16):
    array = jax.random.normal(stream_key, dims, jnp.float32) * spread
    if len(cuts) > 0:
        array = steps_of(stream_key, dims, cuts, -0.22, 0.18) * array
    return jnp.clip(array, min=-bound, max=bound).astype(kind)


def bell_draw_with(stream_key, dims, spread, limit, split, heavy, kind=jnp.bfloat16):
    values = spread * jax.random.normal(stream_key, dims, jnp.float32)
    if split:
        values = values * steps_of(stream_key, dims, split, -0.22, 0.18)
    return jnp.clip(raised(values, jax.random.fold_in(stream_key, 3), *heavy), -limit, limit).astype(kind)


def setup_inputs(seed: int = 0) -> dict:
    key_list = jax.random.split(jax.random.key(seed), 12)
    return {
        "tokens": gaussian(key_list[0], (TOKENS, D), 1.0, 6.0, ((0, 32),)),
        "positions": draw_positions(jax.random.fold_in(key_list[11], 71), 0),
        "norm1_gain": jnp.clip(1.0 + 0.1 * jax.random.normal(key_list[2], (D,), jnp.float32), 0.5, 1.5).astype(jnp.bfloat16),
        "query_weight": gaussian(key_list[3], (D, HQ * HD), D ** -0.5, 0.125, ((0, 16), (1, 2))),
        "kv_weight": gaussian(key_list[4], (D, 2 * HD), D ** -0.5, 0.125, ((0, 16),)),
        "out_weight": gaussian(key_list[5], (D, HQ * HD), (max(HQ * HD // 16, 1)) ** -0.5, 0.5, ((0, 16), (1, 2))),
        "norm2_gain": jnp.clip(1.0 + 0.1 * jax.random.normal(key_list[6], (D,), jnp.float32), 0.5, 1.5).astype(jnp.bfloat16),
        "gate_weight": gaussian(key_list[7], (D, FF), D ** -0.5, 0.125, ((0, 16), (1, 2))),
        "up_weight": gaussian(key_list[8], (D, FF), D ** -0.5, 0.125, ((0, 16), (1, 2))),
        "down_weight": gaussian(key_list[9], (D, FF), FF ** -0.5, 0.0625, ((0, 16), (1, 2))),
        "cotangent": bell_draw_with(key_list[10], (TOKENS, D), 1.0, 6.0, ((0, 32),), (0, 1, 32, 2.75)),
    }


EPSILON = 1e-06
GELU_SCALE = 0.7978845608028654
ROPE_BASE = 10000.0
NEGATIVE = -1e+30

@jax.custom_vjp
def low(v):
    return lax.optimization_barrier(v.astype(jnp.bfloat16)).astype(jnp.float32)

@jax.custom_vjp
def low_back(v):
    return v

def low_keep(v):
    return (low(v), None)

def low_pass(kept, grad):
    return (grad,)

def back_keep(v):
    return (v, None)

def back_low(kept, grad):
    return (low(grad),)
low.defvjp(low_keep, low_pass)
low_back.defvjp(back_keep, back_low)

def rope_tables(positions, head_size):
    quarter = head_size // 4
    ladder = jnp.arange(quarter, dtype=jnp.float32)
    inverse = ROPE_BASE ** (-ladder / quarter)
    angles = positions.astype(jnp.float32)[:, None] * inverse[None, :]
    return (jnp.cos(angles)[:, None, :], jnp.sin(angles)[:, None, :])

def rotate(tensor, cosine_table, sine_table):
    quarter = tensor.shape[-1] // 4
    leading = tensor[..., :quarter]
    trailing = tensor[..., quarter:2 * quarter]
    return jnp.concatenate([leading * cosine_table - trailing * sine_table, trailing * cosine_table + leading * sine_table, tensor[..., 2 * quarter:]], axis=-1)

def geglu(gate_value, up_value):
    cubic_term = gate_value + 0.044715 * gate_value * gate_value * gate_value
    return 0.5 * gate_value * (1.0 + jnp.tanh(GELU_SCALE * cubic_term)) * up_value

def matmul(first_op, second_op):
    return jnp.dot(first_op, second_op, precision=lax.Precision.HIGHEST, preferred_element_type=jnp.float32)

def rms_normal(tensor):
    return tensor * lax.rsqrt(lax.optimization_barrier(jnp.mean(tensor * tensor, axis=-1, keepdims=True)) + EPSILON)

def reference(tokens, positions, norm1_gain, query_weight, kv_weight, out_weight, norm2_gain, gate_weight, up_weight, down_weight, cotangent):
    cosine_table, sine_table = rope_tables(positions, HD)
    query_scale = HD ** (-0.5)
    block_rows = 4 * TOK_W
    back_rows = REACH * TOK_W
    block_count = TOKENS // block_rows

    def attention(queries, keys, values):
        zeros_front = jnp.zeros((back_rows, HD), jnp.float32)
        keys_padded = jnp.concatenate([zeros_front, keys], axis=0)
        values_padded = jnp.concatenate([zeros_front, values], axis=0)

        def one_block(block_index):
            start_row = block_index * block_rows
            query_block = lax.dynamic_slice_in_dim(queries, start_row, block_rows, 0)
            key_block = lax.dynamic_slice_in_dim(keys_padded, start_row, block_rows + back_rows, 0)
            value_block = lax.dynamic_slice_in_dim(values_padded, start_row, block_rows + back_rows, 0)
            place_block = lax.dynamic_slice_in_dim(positions, start_row, block_rows, 0)
            distance = jnp.arange(block_rows, dtype=jnp.int32)[:, None] + back_rows - jnp.arange(block_rows + back_rows, dtype=jnp.int32)[None, :]
            visible = (distance >= 0) & (distance <= place_block[:, None]) & (distance < WINDOW)
            scores = low_back(jnp.einsum('qhd,kd->hqk', query_block, key_block, precision=lax.Precision.HIGHEST))
            masked = jnp.where(visible[None], scores, NEGATIVE)
            highest = lax.optimization_barrier(jnp.max(masked, axis=-1, keepdims=True))
            weights = jnp.exp(masked - highest)
            probs = weights / lax.optimization_barrier(jnp.sum(weights, axis=-1, keepdims=True))
            mixed = jnp.einsum('hqk,kd->qhd', low(probs), value_block, precision=lax.Precision.HIGHEST)
            return mixed.reshape(block_rows, HQ * HD)
        blocks = lax.map(jax.checkpoint(one_block), jnp.arange(block_count, dtype=jnp.int32))
        return blocks.reshape(TOKENS, HQ * HD)

    def forward(inputs, gain_one, query_w, kv_w, out_w, gain_two, gate_w, up_w, down_w):
        normal_one = rms_normal(inputs)
        normed_one = low(normal_one * gain_one)
        query_raw = low_back(matmul(normed_one, query_w)).reshape(TOKENS, HQ, HD)
        kv_raw = low_back(matmul(normed_one, kv_w))
        queries = low(rotate(query_raw, cosine_table, sine_table) * query_scale)
        keys = low(rotate(kv_raw[:, None, :HD], cosine_table, sine_table)[:, 0, :])
        values = low(kv_raw[:, HD:])
        attended = low_back(low(attention(queries, keys, values)))
        residual = inputs + low_back(matmul(attended, out_w.T))
        normal_two = rms_normal(residual)
        normed_two = low(normal_two * gain_two)
        gate_value = low_back(matmul(normed_two, gate_w))
        up_value = low_back(matmul(normed_two, up_w))
        hidden = low(geglu(gate_value, up_value))
        return residual + matmul(hidden, down_w.T)
    result, pull = jax.vjp(forward, tokens.astype(jnp.float32), norm1_gain.astype(jnp.float32), query_weight.astype(jnp.float32), kv_weight.astype(jnp.float32), out_weight.astype(jnp.float32), norm2_gain.astype(jnp.float32), gate_weight.astype(jnp.float32), up_weight.astype(jnp.float32), down_weight.astype(jnp.float32))
    grads = pull(cotangent.astype(jnp.float32))
    return (result.astype(jnp.bfloat16), grads[0].astype(jnp.bfloat16), grads[1], grads[2], grads[3], grads[4], grads[5], grads[6], grads[7], grads[8])
```

```python
import jax
import jax.numpy as jnp
from jax import lax
from jax.sharding import PartitionSpec as P

WINDOW = 2048
MAXLEN = 2048
GROUP = 4


EPSILON = 1e-06
GELU_SCALE = 0.7978845608028654
ROPE_BASE = 10000.0
NEGATIVE = -1e30


def low(array):
    return array.astype(jnp.bfloat16)


def wide_up(array):
    return array.astype(jnp.float32)


def passed_along(array, by):
    length = lax.axis_size("wide")
    pairs = [(i, i + by) for i in range(length) if 0 <= i + by < length]
    return lax.ppermute(array, "wide", pairs)


def crossed(array, mask):
    length = lax.axis_size("wide")
    return lax.ppermute(array, "wide", [(i, i ^ mask) for i in range(length)])


def ringed(array, by):
    length = lax.axis_size("wide")
    return lax.ppermute(array, "wide", [(i, (i + by * GROUP) % length) for i in range(length)])


def swapped(array):
    return lax.ppermute(array, "tp", [(0, 1), (1, 0)])


def rope_tables(positions, head_size):
    quarter = head_size // 4
    ladder = jnp.arange(quarter, dtype=jnp.float32)
    inverse = ROPE_BASE ** (-ladder / quarter)
    angles = positions.astype(jnp.float32)[:, None] * inverse[None, :]
    return (jnp.cos(angles)[:, None, :], jnp.sin(angles)[:, None, :])


def rotate(tensor, cosine_table, sine_table):
    quarter = tensor.shape[-1] // 4
    leading = tensor[..., :quarter]
    trailing = tensor[..., quarter : 2 * quarter]
    return jnp.concatenate(
        [
            leading * cosine_table - trailing * sine_table,
            trailing * cosine_table + leading * sine_table,
            tensor[..., 2 * quarter :],
        ],
        axis=-1,
    )


def geglu(gate_value, up_value):
    cubic_term = gate_value + 0.044715 * gate_value * gate_value * gate_value
    return 0.5 * gate_value * (1.0 + jnp.tanh(GELU_SCALE * cubic_term)) * up_value


def rms_forward(tensor, gain_row):
    inv_rms = lax.rsqrt(jnp.mean(tensor * tensor, axis=-1, keepdims=True) + EPSILON)
    normal = tensor * inv_rms
    return (normal, inv_rms, low(normal * wide_up(gain_row)))


def rms_backward(grad_normed, normal, inv_rms, gain_row):
    scaled = grad_normed * wide_up(gain_row)
    inner_mean = jnp.mean(scaled * normal, axis=-1, keepdims=True)
    return (inv_rms * (scaled - normal * inner_mean), jnp.sum(grad_normed * normal, axis=0))


def cross_rows(first_op, second_op):
    return lax.dot_general(
        first_op, second_op, (((0,), (0,)), ((), ())), preferred_element_type=jnp.float32
    )


def against(first_op, second_op):
    return lax.dot_general(
        first_op, second_op, (((1,), (1,)), ((), ())), preferred_element_type=jnp.float32
    )


def product(first_op, second_op):
    return jnp.dot(first_op, second_op, preferred_element_type=jnp.float32)


def pair_rows(local_rows):
    return jnp.concatenate([local_rows, swapped(local_rows)], axis=0)


def pair_sum(partial):
    half = partial.shape[0] // 2
    return partial[:half] + swapped(partial[half:])


def group_gather(rows):
    half = rows.shape[0] // 2
    one = crossed(rows, 1)
    two = crossed(rows, 2)
    three = jnp.concatenate([crossed(two[:half], 1), crossed(one[half:], 2)], axis=0)
    return [rows, one, two, three]


def group_sum(pieces):
    own, one, two, three = pieces
    half = own.shape[0] // 2
    relay_one = wide_up(crossed(low(three[:half]), 2))
    relay_two = wide_up(crossed(low(three[half:]), 1))
    to_one = jnp.concatenate([low(one[:half] + relay_one), low(one[half:])], axis=0)
    to_two = jnp.concatenate([low(two[:half]), low(two[half:] + relay_two)], axis=0)
    return own + wide_up(crossed(to_one, 1)) + wide_up(crossed(to_two, 2))


def after(array, *others):
    return lax.optimization_barrier((array, *others))[0]


def spread(shard, ring, ring_at, lane):
    rows, cols = shard.shape
    whole = jnp.zeros((ring * GROUP * rows, cols), shard.dtype)
    blocks = [shard]
    for _ in range(1, ring):
        blocks.append(ringed(blocks[-1], -1))
    arrived = None
    for step, block in enumerate(blocks):
        if arrived is not None:
            block = after(block, arrived)
        pieces = group_gather(block)
        arrived = pieces[1]
        at = ((ring_at + step) % ring) * GROUP
        for mask in range(GROUP):
            whole = lax.dynamic_update_slice(
                whole, pieces[mask], ((at + (lane ^ mask)) * rows, 0)
            )
    return whole, blocks[1 % ring], blocks[-1]


def collect(partial, ring, ring_at, lane):
    rows = partial.shape[0] // (ring * GROUP)
    split = partial.reshape(ring, GROUP, rows, partial.shape[1])
    pieces = [
        lax.dynamic_index_in_dim(split, lane ^ mask, 1, keepdims=False) for mask in range(GROUP)
    ]
    summed = group_sum(pieces)

    def block(step):
        return lax.dynamic_index_in_dim(summed, (ring_at + step) % ring, 0, keepdims=False)

    moving = block(1 % ring)
    for step in range(1, ring):
        moving = wide_up(ringed(low(moving), -1)) + block((step + 1) % ring)
    return moving


def local(
    tokens,
    positions,
    norm1_gain,
    query_weight,
    kv_weight,
    out_weight,
    norm2_gain,
    gate_weight,
    up_weight,
    down_weight,
    cotangent,
):
    wide = lax.axis_size("wide")
    ring = wide // GROUP
    me = lax.axis_index("wide")
    core = lax.axis_index("tp")
    lane = me % GROUP
    ring_at = me // GROUP
    first_core = core == 0
    wide_rows = positions.shape[0]
    core_rows = wide_rows // 2
    head_size = kv_weight.shape[1] // 2
    query_cols = query_weight.shape[1]
    local_heads = query_cols // head_size
    model_width = tokens.shape[1]
    ff_local = gate_weight.shape[1]
    ff_part = -(-ff_local // (GROUP * 128)) * 128
    reach_blocks = (MAXLEN - 1) // wide_rows + 1
    key_count = (reach_blocks + 1) * wide_rows
    query_scale = head_size ** (-0.5)
    own_rows = model_width // wide
    ring_rows = GROUP * own_rows

    def part_start(place):
        return jnp.minimum(place * ff_part, ff_local - ff_part)

    def core_order(rows):
        turned = jnp.concatenate([rows[core_rows:], rows[:core_rows]], axis=0)
        return jnp.where(first_core, rows, turned)

    own_positions = core_order(positions)
    cosine_table, sine_table = rope_tables(own_positions, head_size)

    gains = jnp.zeros((2, model_width), jnp.bfloat16)
    gains = lax.dynamic_update_slice(
        gains, jnp.stack([norm1_gain, norm2_gain]), (0, me * own_rows)
    )
    mask = 1
    while mask < wide:
        gains = gains + crossed(gains, mask)
        mask *= 2
    gain_one, gain_two = gains[0], gains[1]

    kv_half = lax.dynamic_slice_in_dim(kv_weight, core * head_size, head_size, 1)
    query_kv_full, query_kv_first, query_kv_last = spread(
        jnp.concatenate([query_weight, kv_half], axis=1), ring, ring_at, lane
    )
    query_full = query_kv_full[:, :query_cols]
    kv_full = query_kv_full[:, query_cols:]
    out_full, _, out_last = spread(after(out_weight, query_kv_last), ring, ring_at, lane)

    def units(weight):
        block = jnp.zeros((ring_rows, ff_part), weight.dtype)
        for mask in range(GROUP):
            other = lane ^ mask
            piece = lax.dynamic_slice_in_dim(weight, part_start(other), ff_part, 1)
            kept = part_start(other) + jnp.arange(ff_part) >= other * ff_part
            piece = jnp.where(kept[None, :], piece, jnp.zeros_like(piece))
            if mask > 0:
                piece = crossed(piece, mask)
            block = lax.dynamic_update_slice(block, piece, (other * own_rows, 0))
        return block

    def rung(block, starts):
        whole = jnp.zeros((model_width, ff_part), block.dtype)
        passed = [block]
        for step in range(ring):
            if step > 0:
                block = ringed(after(block, starts[-2]), -1)
                starts.append(block)
            whole = lax.dynamic_update_slice(
                whole, block, (((ring_at + step) % ring) * ring_rows, 0)
            )
        return whole

    gate_block = units(after(gate_weight, query_kv_first))
    up_block = units(after(up_weight, query_kv_full))
    down_block = units(after(down_weight, up_block))
    starts = [query_kv_last, query_kv_last]
    gate_part = rung(gate_block, starts)
    up_part = rung(up_block, starts)
    down_part = rung(down_block, starts)

    def group_rows(rows):
        return pair_rows(jnp.concatenate(group_gather(rows), axis=0))

    def group_rows_sum(partial):
        mine = pair_sum(partial)
        return group_sum([mine[i * core_rows : (i + 1) * core_rows] for i in range(GROUP)])

    grad_rows = group_rows(after(cotangent, out_full))

    inputs = wide_up(tokens)
    normal_one, inv_rms_one, normed_one = rms_forward(inputs, gain_one)
    rows_one = pair_rows(normed_one)
    query_raw = product(rows_one, query_full).reshape(wide_rows, local_heads, head_size)
    queries = low(rotate(query_raw, cosine_table, sine_table) * query_scale)
    half_raw = product(rows_one, kv_full)
    half_turned = rotate(half_raw[:, None, :], cosine_table, sine_table)[:, 0, :]
    half_own = core_order(low(jnp.where(first_core, half_turned, half_raw)))
    blocks = [half_own]
    for offset in range(1, reach_blocks + 1):
        blocks.append(passed_along(half_own, offset))
    half_window = jnp.concatenate(blocks[::-1], axis=0)
    other_window = swapped(half_window)
    keys_all = jnp.where(first_core, half_window, other_window)
    values_all = jnp.where(first_core, other_window, half_window)
    row_places = (jnp.arange(wide_rows) + core * core_rows) % wide_rows
    distance = row_places[:, None] + reach_blocks * wide_rows - jnp.arange(key_count)[None, :]
    visible = (distance >= 0) & (distance <= own_positions[:, None]) & (distance < WINDOW)
    scores = jnp.einsum("qhd,kd->hqk", queries, keys_all, preferred_element_type=jnp.float32)
    masked = jnp.where(visible[None], scores, NEGATIVE)
    highest = jnp.max(masked, axis=-1, keepdims=True)
    weights = jnp.exp(masked - highest)
    totals = jnp.sum(weights, axis=-1, keepdims=True)
    log_totals = highest + jnp.log(totals)
    probs_low = low(weights / totals)
    attended = jnp.einsum("hqk,kd->qhd", probs_low, values_all, preferred_element_type=jnp.float32)
    attended = low(attended.reshape(wide_rows, query_cols))
    residual = inputs + pair_sum(against(attended, out_full))

    normal_two, inv_rms_two, normed_two = rms_forward(residual, gain_two)
    rows_two = group_rows(normed_two)
    gate_value = product(rows_two, gate_part)
    up_value = product(rows_two, up_part)
    hidden = low(geglu(gate_value, up_value))
    output = low(residual + group_rows_sum(against(hidden, down_part)))
    grad_hidden = product(grad_rows, down_part)
    pull_hidden = jax.vjp(geglu, gate_value, up_value)[1]
    grad_gate, grad_up = pull_hidden(grad_hidden)
    grad_gate = low(grad_gate)
    grad_up = low(grad_up)
    grad_normed_two = group_rows_sum(against(grad_gate, gate_part) + against(grad_up, up_part))
    grad_residual_norm, gain_two_term = rms_backward(
        grad_normed_two, normal_two, inv_rms_two, gain_two
    )
    grad_residual = wide_up(cotangent) + grad_residual_norm
    grad_branch = low(grad_residual)

    def owned(rows, grads):
        def block(step):
            start = ((ring_at + step) % ring) * ring_rows
            return cross_rows(lax.dynamic_slice_in_dim(rows, start, ring_rows, 1), grads)

        moving = block(1 % ring)
        for step in range(1, ring):
            moving = wide_up(ringed(low(moving), -1)) + block((step + 1) % ring)
        parts = []
        for mask in range(GROUP):
            piece = lax.dynamic_slice_in_dim(moving, (lane ^ mask) * own_rows, own_rows, 0)
            parts.append(wide_up(crossed(low(piece), mask)) if mask > 0 else piece)
        placed = [lax.select_n(lane ^ place, *parts) for place in range(GROUP)]
        skipped = GROUP * ff_part - ff_local
        placed[-1] = placed[-1][:, skipped:]
        return jnp.concatenate(placed, axis=1)

    grad_gate_weight = owned(rows_two, grad_gate)
    grad_up_weight = owned(rows_two, grad_up)
    grad_down_weight = owned(grad_rows, hidden)

    branch_full = pair_rows(grad_branch)
    grad_out_weight = collect(cross_rows(branch_full, attended), ring, ring_at, lane)
    grad_attended = low(product(branch_full, out_full))
    grad_attended = grad_attended.reshape(wide_rows, local_heads, head_size)
    scores_again = jnp.einsum("qhd,kd->hqk", queries, keys_all, preferred_element_type=jnp.float32)
    probs_full = jnp.exp(jnp.where(visible[None], scores_again, NEGATIVE) - log_totals)
    grad_probs = jnp.einsum(
        "qhd,kd->hqk", grad_attended, values_all, preferred_element_type=jnp.float32
    )
    inner_sums = jnp.sum(probs_full * grad_probs, axis=-1, keepdims=True)
    grad_scores = low(probs_full * (grad_probs - inner_sums))
    grad_queries = jnp.einsum(
        "hqk,kd->qhd", grad_scores, keys_all, preferred_element_type=jnp.float32
    )
    grad_keys = jnp.einsum("hqk,qhd->kd", grad_scores, queries, preferred_element_type=jnp.float32)
    grad_values = jnp.einsum(
        "hqk,qhd->kd",
        low(probs_full),
        grad_attended,
        preferred_element_type=jnp.float32,
    )
    half_kept = jnp.where(first_core, grad_keys, grad_values)
    half_given = jnp.where(first_core, grad_values, grad_keys)
    half_grads = half_kept + wide_up(swapped(low(half_given)))
    grad_own = half_grads[reach_blocks * wide_rows :]
    for offset in range(1, reach_blocks + 1):
        piece_start = (reach_blocks - offset) * wide_rows
        piece = low(half_grads[piece_start : piece_start + wide_rows])
        grad_own = grad_own + wide_up(passed_along(piece, -offset))
    grad_own = core_order(grad_own)
    grad_turned = rotate(grad_own[:, None, :], cosine_table, -sine_table)[:, 0, :]
    grad_half_raw = low(jnp.where(first_core, grad_turned, grad_own))
    grad_query_raw = low(
        rotate(grad_queries * query_scale, cosine_table, -sine_table).reshape(wide_rows, query_cols)
    )
    grad_query_weight = collect(cross_rows(rows_one, grad_query_raw), ring, ring_at, lane)
    grad_half_weight = collect(cross_rows(rows_one, grad_half_raw), ring, ring_at, lane)
    other_half = swapped(grad_half_weight)
    grad_kv_weight = jnp.where(
        first_core,
        jnp.concatenate([grad_half_weight, other_half], axis=1),
        jnp.concatenate([other_half, grad_half_weight], axis=1),
    )
    grad_normed_one = pair_sum(
        against(grad_query_raw, query_full) + against(grad_half_raw, kv_full)
    )
    grad_input_norm, gain_one_term = rms_backward(
        grad_normed_one, normal_one, inv_rms_one, gain_one
    )
    grad_tokens = low(grad_residual + grad_input_norm)

    def gain_total(term):
        term = term[None]
        term = term + swapped(term)
        mask = 1
        while mask < wide:
            term = term + crossed(term, mask)
            mask *= 2
        return lax.dynamic_slice(term, (0, me * own_rows), (1, own_rows))[0]

    return (
        output,
        grad_tokens,
        gain_total(gain_one_term),
        grad_query_weight,
        grad_kv_weight,
        grad_out_weight,
        gain_total(gain_two_term),
        grad_gate_weight,
        grad_up_weight,
        grad_down_weight,
    )


def solution(mesh):
    return jax.shard_map(
        local,
        mesh=mesh,
        in_specs=(
            P(("wide", "tp"), None),
            P("wide"),
            P("wide"),
            P("wide", "tp"),
            P("wide", None),
            P("wide", "tp"),
            P("wide"),
            P("wide", "tp"),
            P("wide", "tp"),
            P("wide", "tp"),
            P(("wide", "tp"), None),
        ),
        out_specs=(
            P(("wide", "tp"), None),
            P(("wide", "tp"), None),
            P("wide"),
            P("wide", "tp"),
            P("wide", None),
            P("wide", "tp"),
            P("wide"),
            P("wide", "tp"),
            P("wide", "tp"),
            P("wide", "tp"),
        ),
        check_vma=False,
    )
```
